256 devices in a mesh: pb: 8 (over x, core), pa: 32 (over z, y).
Axes of the slice: x: 4, y: 4, z: 8, core: 2. Of those that a mesh axis runs over, the one named last changes fastest.
Arguments:
- query_kv: bfloat16 [256, 2, 32, 1024], P(('pb', 'pa')), may hold values from -20 to 20
- student_query: bfloat16 [256, 1024], P(('pb', 'pa')), may hold values from -6 to 6
- block_holder: int32 [256, 2, 1], P('pb'), may hold values from 0 to 31; in each aligned block of 64 rows (0 to 63, 64 to 127, ..., all dimensions but the last counted through in order) at most 4 rows name the same one
- cand_local: int32 [256, 2, 32], P('pb'), may hold values from 0 to 63, all different within a row
- counts: int32 [256], P('pb'), may hold values from 1 to 64
- passage_qkv: bfloat16 [2048, 3, 32, 1024], P(('pa', 'pb')), may hold values from -20 to 20
- passage_resid: bfloat16 [2048, 1024], P(('pa', 'pb')), may hold values from -6 to 6
- student_passage: bfloat16 [2048, 1024], P(('pa', 'pb')), may hold values from -6 to 6
- w_o: bfloat16 [1024, 1024], replicated, may hold values from -0.1875 to 0.1875
- ln_gain: float32 [1024], replicated, may hold values from 0.5 to 1.5
- ln_bias: float32 [1024], replicated, may hold values from -3 to 3
- w_dense: bfloat16 [1024, 1024], replicated, may hold values from -0.1875 to 0.1875
- b_dense: float32 [1024], replicated, may hold values from -3 to 3
- w_out: float32 [1024], replicated, may hold values from -0.6 to 0.6
Outputs:
- teacher_scores: float32 [256, 64], P(('pb', 'pa'))
- query_loss: float32 [256], P(('pb', 'pa'))
- grad_query: float32 [256, 1024], P(('pb', 'pa'))
- grad_passage: float32 [2048, 1024], P(('pa', 'pb'))
The draws below stay inside these ranges and needn't reach their ends.
Inputs may be any that keep to these rules, and one draw needn't show every extreme that they name: `block_holder`: among the 64 candidate blocks of the queries of one index of pb, padding blocks included, no holder is named more than 4 times; in some index of pb one holder is named exactly 4 times. `cand_local`: the 32 entries of one block are distinct. Slots from counts[q] on are padding.
All inputs are finite; a program needn't handle non-finite values.
Results may differ from the reference program's by a relative error of at most 0.0038.
Values may be sent and summed in bfloat16 or wider, within the bound.
No kernel may reach another device: no remote copies, remote signals or barrier semaphores. Data moves between devices by JAX's collectives and lax.ppermute only.
A program may use at most 128 MiB of HBM per device.

```python
import math
import jax
import jax.numpy as jnp
import numpy as np
from jax import lax

D = 1024
HEADS = 16
Q_LEN = 32
P_LEN = 32
BLOCK = 32
CAND_BLOCKS = 2
P_DEV = 8
HOLD_CAP = 4
POOL = 64
ROW_BLOCKS = 64
QUERIES = 256
PASSAGES = 2048
N_PA = 32


def draw_query_kv(key, part):
    shape = (QUERIES, 2, Q_LEN, D)
    base = jnp.clip(jax.random.normal(jax.random.fold_in(key, 13), shape, jnp.float32), -5.0, 5.0)
    return base.astype(jnp.bfloat16)


def draw_passage_qkv(key, part):
    shape = (PASSAGES, 3, P_LEN, D)
    base = jnp.clip(jax.random.normal(jax.random.fold_in(key, 24), shape, jnp.float32), -5.0, 5.0)
    return base.astype(jnp.bfloat16)


def student_rows(key, salt, count):
    rows = jnp.clip(jax.random.normal(jax.random.fold_in(key, salt + 2), (count, D), jnp.float32), -5.0, 5.0)
    return rows.astype(jnp.bfloat16)


def draw_student_query(key, part):
    return student_rows(key, 31, QUERIES)


def draw_student_passage(key, part):
    return student_rows(key, 41, PASSAGES)


def set_ends(values, key, low, top_value):
    index_at = [jax.random.randint(jax.random.fold_in(key, axis), (), 0, length) for axis, length in enumerate(values.shape)]
    main_axis = values.shape.index(max(values.shape))
    beside = index_at[:main_axis] + [(index_at[main_axis] + 1) % values.shape[main_axis]] + index_at[main_axis + 1:]
    return values.at[tuple(index_at)].set(low).at[tuple(beside)].set(top_value)


def steps_of(own_key, dims, split, smallest, top_value):
    def one(position, shards_of):
        heights = jax.random.uniform(jax.random.fold_in(jax.random.fold_in(own_key, 6), position), (shards_of,), jnp.float32, smallest / len(split), top_value / len(split))
        return jnp.repeat(jnp.exp(heights), dims[position] // shards_of).reshape((-1,) + (1,) * (len(dims) - position - 1))

    loudness = one(*split[0])
    for cut in split[1:]:
        loudness = loudness * one(*cut)
    return loudness


def choose_distinct(key, rows, count, top, lift):
    ranking = jax.random.permutation(jax.random.fold_in(key, 1), count)
    boost = ranking
    for power in range(3):
        boost = boost * boost // count
    boost = boost * lift // count
    lots = jax.random.randint(jax.random.fold_in(key, 2), (rows, count), 0, 4096) + boost
    sure = jax.random.permutation(jax.random.fold_in(key, 3), rows)[jnp.arange(count) % rows]
    lots = jnp.where(jnp.arange(rows)[:, None] == sure[None, :], 1 << 14, lots)
    priority = lots * count + jnp.arange(count)
    return lax.top_k(priority.astype(jnp.int32), top)[1].astype(jnp.int32)


def deal_out(key, own, number, rows, number_of, top, most, lean):
    ranking = jax.random.permutation(key, number_of)
    packed, ordinary = load_shares(number_of, rows * top, most, lean, True), load_shares(number_of, rows * top, most, lean, False)
    places = jnp.arange(number_of)

    def named(tallies, turn):
        used = int((tallies > 0).sum())
        fixed = max(1, used // 4)
        passed = fixed + (places - fixed + turn * (used - fixed)) % max(1, number_of - fixed)
        return jnp.zeros((number_of,), jnp.int32).at[ranking[jnp.where(places < fixed, places, passed)]].set(jnp.asarray(tallies, jnp.int32))

    tallies = jnp.where(number % 4 == 0, named(packed, number // 4), named(ordinary, number - number // 4 - 1))
    mixed = jax.random.permutation(jax.random.fold_in(own, 3), number_of)
    giver, taker = mixed[0:number_of // 2 * 2:2], mixed[1:number_of // 2 * 2:2]
    room = jnp.minimum(tallies[giver] - 1, most - tallies[taker]) // 2
    room = jnp.where((giver == ranking[0]) | (taker == ranking[0]) | (tallies[taker] == 0), 0, jnp.maximum(room, 0))
    passed = jax.random.randint(jax.random.fold_in(own, 4), (number_of // 2,), 0, 1 << 20) % (room + 1)
    tallies = tallies.at[giver].add(-passed).at[taker].add(passed)
    members = jnp.searchsorted(jnp.cumsum(tallies), jnp.arange(rows * top), side="right").astype(jnp.int32)
    table = members.reshape(top, rows).T
    table = table[jax.random.permutation(jax.random.fold_in(own, 1), rows)]
    turn = jax.random.randint(jax.random.fold_in(own, 2), (rows, 1), 0, top)
    return jnp.take_along_axis(table, (jnp.arange(top)[None, :] + turn) % top, axis=1)


def load_shares(number_of, total, limit, lean, full):
    weights = [(1 << 20) // math.isqrt(grade ** lean) + 1 for grade in range(1, number_of + 1)]
    largest = limit if full else min(limit, max(-(-total // number_of), total * weights[0] // sum(weights)))
    least = 1 if total - largest >= number_of - 1 else 0
    given, surplus = [largest] + [least] * (number_of - 1), total - largest - least * (number_of - 1)
    while surplus > 0:
        movable = [i for i in range(1, number_of) if given[i] < largest] or [i for i in range(1, number_of) if given[i] < limit]
        pool, budget = sum([weights[i] for i in movable]), surplus
        for i in movable:
            more = min(limit - given[i], max(1, budget * weights[i] // pool), surplus)
            given[i] = given[i] + more
            surplus = surplus - more
    return np.array(given)


def centred(own_key, shape, scale, reach, cuts=(), held_as=jnp.bfloat16):
    array = jax.random.normal(own_key, shape, jnp.float32) * scale
    if len(cuts) > 0:
        array = steps_of(own_key, shape, cuts, -0.22, 0.18) * array
    return jnp.clip(array, min=-reach, max=reach).astype(held_as)


def setup_inputs(seed: int = 0) -> dict:
    splits = jax.random.split(jax.random.key(seed), 15)
    query_kv = draw_query_kv(jax.random.fold_in(splits[14], 71), 0)
    student_query = draw_student_query(jax.random.fold_in(splits[14], 71), 0)
    block_holder_keys = jax.random.split(jax.random.fold_in(splits[2], 1), QUERIES * CAND_BLOCKS // ROW_BLOCKS)
    block_holder_turns = jax.random.permutation(jax.random.fold_in(splits[2], 3), QUERIES * CAND_BLOCKS // ROW_BLOCKS)
    block_holder = jax.vmap(lambda own, number: deal_out(jax.random.fold_in(splits[2], 2), own, number, ROW_BLOCKS, N_PA, 1, HOLD_CAP, 1))(block_holder_keys, block_holder_turns).reshape((QUERIES, CAND_BLOCKS, 1))
    cand_local = choose_distinct(splits[3], QUERIES * CAND_BLOCKS, POOL, BLOCK, 0).reshape((QUERIES, CAND_BLOCKS, BLOCK))
    counts = set_ends(jax.random.randint(splits[4], (QUERIES,), 1, CAND_BLOCKS * BLOCK + 1), jax.random.fold_in(splits[4], 1), 1, CAND_BLOCKS * BLOCK).astype(jnp.int32)
    passage_qkv = draw_passage_qkv(jax.random.fold_in(splits[14], 71), 0)
    passage_resid = centred(splits[6], (PASSAGES, D), 1.0, 6.0, ((0, 256),))
    student_passage = draw_student_passage(jax.random.fold_in(splits[14], 71), 0)
    w_o = centred(splits[8], (D, D), D ** -0.5, 0.1875)
    ln_gain = jnp.clip(1.0 + 0.1 * jax.random.normal(splits[9], (D,), jnp.float32), 0.5, 1.5)
    ln_bias = centred(splits[10], (D,), 0.5, 3.0, (), jnp.float32)
    w_dense = centred(splits[11], (D, D), D ** -0.5, 0.1875)
    b_dense = centred(splits[12], (D,), 0.5, 3.0, (), jnp.float32)
    w_out = centred(splits[13], (D,), 0.1, 0.6, (), jnp.float32)
    return dict(query_kv=query_kv, student_query=student_query, block_holder=block_holder, cand_local=cand_local, counts=counts, passage_qkv=passage_qkv, passage_resid=passage_resid, student_passage=student_passage, w_o=w_o, ln_gain=ln_gain, ln_bias=ln_bias, w_dense=w_dense, b_dense=b_dense, w_out=w_out)


student_scale = 0.125
norm_eps = 1e-05

def self_attend(block_qkv):
    passage_count, _, length, feature_width = block_qkv.shape
    head_dim = feature_width // HEADS
    split_qkv = block_qkv.reshape(passage_count, 3, length, HEADS, head_dim).astype(jnp.float32)
    scores = jnp.einsum('pthd,puhd->phtu', split_qkv[:, 0], split_qkv[:, 1]) * head_dim ** (-0.5)
    row_max = lax.optimization_barrier(jnp.max(scores, axis=-1, keepdims=True))
    scaled = jnp.exp(scores - row_max)
    row_total = lax.optimization_barrier(jnp.sum(scaled, axis=-1, keepdims=True))
    self_lse = (row_max + jnp.log(row_total))[..., 0]
    self_probs = (scaled / row_total).astype(jnp.bfloat16)
    self_out = jnp.einsum('phtu,puhd->pthd', self_probs.astype(jnp.float32), split_qkv[:, 2])
    return (self_out.reshape(passage_count, length, feature_width).astype(jnp.bfloat16), self_lse)

def score_block(pass_q, pass_o, pass_lse, pass_resid, key_val, weights):
    w_o, ln_gain, ln_bias, w_dense, b_dense, w_out = weights
    passage_count, length, feature_width = pass_q.shape
    head_dim = feature_width // HEADS
    query_len = key_val.shape[1]
    token_rows = pass_q.reshape(passage_count * length, HEADS, head_dim).astype(jnp.float32)
    key_rows = key_val[0].reshape(query_len, HEADS, head_dim).astype(jnp.float32)
    value_rows = key_val[1].reshape(query_len, HEADS, head_dim).astype(jnp.float32)
    scores = jnp.einsum('rhd,ahd->har', token_rows, key_rows) * head_dim ** (-0.5)
    row_max = lax.optimization_barrier(jnp.max(scores, axis=1, keepdims=True))
    scaled = jnp.exp(scores - row_max)
    row_total = lax.optimization_barrier(jnp.sum(scaled, axis=1, keepdims=True))
    cross_lse = row_max[:, 0, :] + jnp.log(row_total[:, 0, :])
    self_lse = jnp.transpose(pass_lse, (1, 0, 2)).reshape(HEADS, passage_count * length)
    self_share = jax.nn.sigmoid(self_lse - cross_lse)
    spread = (1.0 - self_share)[:, None, :] * scaled / row_total
    key_weight = (lax.optimization_barrier(jnp.sum(spread.reshape(HEADS, query_len, passage_count, length), axis=3)) / length).astype(jnp.bfloat16)
    query_part = jnp.einsum('hab,ahd->bhd', key_weight.astype(jnp.float32), value_rows).reshape(passage_count, feature_width)
    token_weight = (self_share / length).astype(jnp.bfloat16).reshape(HEADS, passage_count, length)
    self_rows = pass_o.reshape(passage_count, length, HEADS, head_dim).astype(jnp.float32)
    self_part = jnp.einsum('hbt,bthd->bhd', token_weight.astype(jnp.float32), self_rows).reshape(passage_count, feature_width)
    pooled = (query_part + self_part).astype(jnp.bfloat16)
    mixed_rows = jnp.dot(pooled, w_o, preferred_element_type=jnp.float32) + pass_resid.astype(jnp.float32)
    row_mean = lax.optimization_barrier(jnp.mean(mixed_rows, axis=-1, keepdims=True))
    centered = mixed_rows - row_mean
    row_var = lax.optimization_barrier(jnp.mean(centered * centered, axis=-1, keepdims=True))
    normed = (centered * lax.rsqrt(row_var + norm_eps) * ln_gain + ln_bias).astype(jnp.bfloat16)
    hidden = jnp.tanh(jnp.dot(normed, w_dense, preferred_element_type=jnp.float32) + b_dense)
    return lax.optimization_barrier(jnp.sum(hidden * w_out, axis=-1))

def log_probs(scores, is_valid):
    masked = jnp.where(is_valid, scores, jnp.float32(-1e+30))
    row_max = lax.optimization_barrier(jnp.max(masked, axis=-1, keepdims=True))
    scaled = jnp.where(is_valid, jnp.exp(masked - row_max), jnp.float32(0.0))
    return scores - row_max - jnp.log(lax.optimization_barrier(jnp.sum(scaled, axis=-1, keepdims=True)))

def distill(teacher, student, is_valid):
    log_t = log_probs(teacher, is_valid)
    log_s = log_probs(student, is_valid)
    prob_t = jnp.where(is_valid, jnp.exp(log_t), jnp.float32(0.0))
    prob_s = jnp.where(is_valid, jnp.exp(log_s), jnp.float32(0.0))
    loss = lax.optimization_barrier(jnp.sum(jnp.where(is_valid, prob_t * (log_t - log_s), jnp.float32(0.0)), axis=-1))
    return (loss, prob_s - prob_t)

def reference(query_kv, student_query, block_holder, cand_local, counts, passage_qkv, passage_resid, student_passage, w_o, ln_gain, ln_bias, w_dense, b_dense, w_out):
    weights = (w_o, ln_gain, ln_bias, w_dense, b_dense, w_out)
    passage_total = passage_qkv.shape[0]
    groups = passage_qkv.reshape(passage_total // P_DEV, P_DEV, 3, P_LEN, D)
    self_outs, self_lses = lax.map(self_attend, groups)
    all_out = self_outs.reshape(passage_total, P_LEN, D)
    all_lse = self_lses.reshape(passage_total, HEADS, P_LEN)
    all_q = passage_qkv[:, 0]
    passage_ids = (block_holder[:, :, 0][:, :, None] * POOL + cand_local).astype(jnp.int32)

    def per_query(slot_item):
        key_val, query_embed, id_rows = slot_item

        def per_block(id_row):
            teacher = score_block(all_q[id_row], all_out[id_row], all_lse[id_row], passage_resid[id_row], key_val, weights)
            student = student_scale * jnp.dot(student_passage[id_row], query_embed, preferred_element_type=jnp.float32)
            return (teacher, student)
        teacher, student = lax.map(per_block, id_rows)
        return (teacher.reshape(-1), student.reshape(-1))
    teacher_raw, student_raw = lax.map(per_query, (query_kv, student_query, passage_ids))
    slot_count = CAND_BLOCKS * BLOCK
    is_valid = jnp.arange(slot_count, dtype=jnp.int32)[None, :] < counts[:, None]
    query_loss, score_grad = distill(teacher_raw, student_raw, is_valid)
    teacher_scores = jnp.where(is_valid, teacher_raw, jnp.float32(0.0))
    flat_ids = passage_ids.reshape(passage_ids.shape[0], slot_count)
    cand_embed = student_passage[flat_ids].astype(jnp.float32)
    grad_query = student_scale * jnp.einsum('qc,qcd->qd', score_grad, cand_embed, precision=lax.Precision.HIGHEST)
    terms = (score_grad[:, :, None] * student_query[:, None, :].astype(jnp.float32)).reshape(-1, D)
    grad_passage = student_scale * jax.ops.segment_sum(terms, flat_ids.reshape(-1), num_segments=passage_total)
    return (teacher_scores, query_loss, grad_query, grad_passage)
```

```python
import jax
import jax.numpy as jnp
from jax import lax
from jax.experimental import pallas as pl
from jax.experimental.pallas import tpu as pltpu
from jax.sharding import Mesh
from jax.sharding import PartitionSpec as P

PA = ("pa_0", "pa_1")
PB_PA = ("pb", "pa_0", "pa_1")
PA_PB = ("pa_0", "pa_1", "pb")
HOLD_CAP = 4
NG = 8
NZ = 8
NY = 4
NA = NZ * NY
LANES = 128
HALF = 64
PDEV = 8
POOL = 64
TOK = 32
ROWS = PDEV * TOK
SLOTS = NG * HOLD_CAP
FEAT = 1024
SENT = 2 * ROWS + 2 * POOL + 16
KVW = 1152
STEP = 8

student_scale = 0.125
norm_eps = 1e-05
low_score = -1e30

f32 = jnp.float32
bf16 = jnp.bfloat16
NT = (((1,), (1,)), ((), ()))


def exchange(blocks, axis):
    return lax.all_to_all(blocks, axis, split_axis=0, concat_axis=0, tiled=True)


def to_all(shard, axis):
    return exchange(jnp.broadcast_to(shard, (lax.axis_size(axis), *shard.shape)), axis)


def dot32(a, b):
    return jnp.dot(a, b, preferred_element_type=f32)


def dot_exact(a, b):
    return jnp.dot(a, b, preferred_element_type=f32, precision=lax.Precision.HIGHEST)


def first_head(shape):
    return lax.broadcasted_iota(jnp.int32, shape, len(shape) - 1) < HALF


def self_kernel(qkv_ref, resid_ref, student_ref, out_ref):
    q = (qkv_ref[:, 0].astype(f32) * 0.125).astype(bf16).reshape(ROWS, LANES)
    k = qkv_ref[:, 1].reshape(ROWS, LANES)
    v = qkv_ref[:, 2].reshape(ROWS, LANES)
    head0 = first_head((ROWS, LANES))
    zero = jnp.zeros((ROWS, LANES), bf16)
    same = (
        lax.broadcasted_iota(jnp.int32, (ROWS, ROWS), 0) // TOK
        == lax.broadcasted_iota(jnp.int32, (ROWS, ROWS), 1) // TOK
    )
    outs, lses = [], []
    for e in range(2):
        qe = jnp.where(head0 if e == 0 else ~head0, q, zero)
        s = lax.dot_general(qe, k, NT, preferred_element_type=f32)
        s = jnp.where(same, s, low_score)
        m = jnp.max(s, axis=1, keepdims=True)
        p = jnp.exp(s - m)
        total = jnp.sum(p, axis=1, keepdims=True)
        lses.append(m + jnp.log(total))
        outs.append(dot32((p * (1.0 / total)).astype(bf16), v))
    out = jnp.where(head0, outs[0], outs[1]).astype(bf16)
    lse = jnp.where(head0, lses[0], lses[1]).T
    pair = jnp.concatenate(
        [lse[:1, :LANES], lse[:1, LANES:], lse[HALF : HALF + 1, :LANES], lse[HALF : HALF + 1, LANES:]], axis=0
    )
    top = pair.astype(bf16).astype(f32)
    mid = (pair - top).astype(bf16).astype(f32)
    low = pair - top - mid
    out_ref[0, :ROWS, :] = q
    out_ref[0, ROWS : 2 * ROWS, :] = out
    at = 2 * ROWS
    pieces = [r[:, t * LANES : (t + 1) * LANES].astype(f32) for r in (resid_ref, student_ref) for t in range(8)]
    out_ref[0, at : at + 2 * POOL, :] = jnp.concatenate(pieces, axis=0).astype(bf16)
    at += 2 * POOL
    out_ref[0, at : at + 16, :] = jnp.concatenate([top, mid, low, jnp.zeros((4, LANES), f32)], axis=0).astype(bf16)


def cross_kernel(x_ref, kv_ref, out_ref, kw_ref, sp_ref):
    keys, values = [], []
    for z in range(4):
        for r in range(8):
            keys.append(kv_ref[z, 0, :, r * LANES : (r + 1) * LANES].astype(f32))
            values.append(kv_ref[4 + z, 0, :, r * LANES : (r + 1) * LANES].astype(f32))
    k = jnp.concatenate(keys, axis=0)
    v = jnp.concatenate(values, axis=0)
    head0 = first_head((ROWS, LANES))
    ke = [jnp.where(head0, k, 0.0).astype(bf16), jnp.where(head0, 0.0, k).astype(bf16)]
    ve = [jnp.where(head0, v, 0.0).astype(bf16), jnp.where(head0, 0.0, v).astype(bf16)]
    kw_ref[...] = jnp.zeros(kw_ref.shape, f32)
    own_tok = (
        lax.broadcasted_iota(jnp.int32, (PDEV, ROWS), 1) // TOK
        == lax.broadcasted_iota(jnp.int32, (PDEV, ROWS), 0)
    ).astype(f32)
    spread_row = lax.broadcasted_iota(jnp.int32, (ROWS, LANES), 0) // TOK
    spread_col = lax.broadcasted_iota(jnp.int32, (ROWS, LANES), 1)
    head0_sp = first_head((STEP * PDEV, LANES))

    def chunk(c, carry):
        q = x_ref[c, :ROWS, :]
        o = x_ref[c, ROWS : 2 * ROWS, :]
        parts = x_ref[c, 2 * ROWS + 2 * POOL :, :].astype(f32)
        lse = parts[:4] + parts[4:8] + parts[8:12]
        fold = (spread_col == spread_row + c * PDEV).astype(bf16)
        sps = []
        for e in range(2):
            s = lax.dot_general(ke[e], q, NT, preferred_element_type=f32).reshape(TOK, STEP, ROWS)
            m = jnp.max(s, axis=0)
            p = jnp.exp(s - m[None])
            total = jnp.sum(p, axis=0)
            self_lse = jnp.concatenate([lse[2 * e : 2 * e + 1], lse[2 * e + 1 : 2 * e + 2]], axis=1)
            share = 1.0 / (1.0 + jnp.exp(m + jnp.log(total) - self_lse))
            w = (1.0 - share) / (TOK * total)
            pw = (p * w[None]).reshape(STEP * TOK, ROWS).astype(bf16)
            kw_ref[e] += dot32(pw, fold)
            share = share * (1.0 / TOK)
            a = jnp.concatenate([share[j : j + 1] * own_tok for j in range(STEP)], axis=0).astype(bf16)
            sps.append(dot32(a, o))
        sp = jnp.where(head0_sp, sps[0], sps[1]).reshape(STEP, PDEV, LANES)
        sp_ref[:, pl.ds(pl.multiple_of(c * PDEV, PDEV), PDEV), :] = sp
        return carry

    lax.fori_loop(0, NG, chunk, 0)
    col_slot = lax.broadcasted_iota(jnp.int32, (POOL, ROWS), 1) % STEP
    both = jnp.zeros((STEP * POOL, LANES), f32)
    for e in range(2):
        t = kw_ref[e].T[:POOL]
        rows = jnp.concatenate([jnp.where(col_slot == j, t, 0.0) for j in range(STEP)], axis=0).astype(bf16)
        both = both + dot32(rows, ve[e])
    pooled = both.reshape(STEP, POOL, LANES) + sp_ref[...]
    out_ref[...] = pooled.reshape(STEP // HOLD_CAP, HOLD_CAP, POOL, LANES).astype(bf16)


def head_kernel(pr_ref, rs_ref, sq_ref, valid_ref, wo_ref, wd_ref, gain_ref, bias_ref, bd_ref, wout_ref, out_ref):
    n = HOLD_CAP * POOL
    pooled = jnp.concatenate([pr_ref[t] for t in range(8)], axis=1)
    resid = jnp.concatenate(
        [rs_ref[:, t * PDEV : (t + 1) * PDEV, :].astype(f32).reshape(POOL, LANES) for t in range(8)], axis=1
    )
    pool_student = jnp.concatenate(
        [rs_ref[:, POOL + t * PDEV : POOL + (t + 1) * PDEV, :].astype(f32).reshape(POOL, LANES) for t in range(8)],
        axis=1,
    ).astype(bf16)
    mixed = (dot32(pooled, wo_ref[...]).reshape(HOLD_CAP, POOL, FEAT) + resid[None]).reshape(n, FEAT)
    mean = jnp.mean(mixed, axis=1, keepdims=True)
    centered = mixed - mean
    var = jnp.mean(centered * centered, axis=1, keepdims=True)
    normed = (centered * lax.rsqrt(var + norm_eps) * gain_ref[...] + bias_ref[...]).astype(bf16)
    hidden = jnp.tanh(dot32(normed, wd_ref[...]) + bd_ref[...])
    teacher = jnp.sum(hidden * wout_ref[...], axis=1, keepdims=True)
    row = jnp.broadcast_to(teacher, (n, LANES)).T[:1]
    table = jnp.concatenate([row[:, j * POOL : (j + 1) * POOL] for j in range(HOLD_CAP)], axis=0)
    student = student_scale * lax.dot_general(sq_ref[...], pool_student, NT, preferred_element_type=f32)
    table = jnp.where(valid_ref[...] > 0.0, table, low_score)
    out_ref[...] = jnp.concatenate([table, student], axis=1)


def log_probs(scores, valid):
    masked = jnp.where(valid, scores, low_score)
    top = jnp.max(masked, axis=-1, keepdims=True)
    scaled = jnp.where(valid, jnp.exp(masked - top), 0.0)
    return masked - top - jnp.log(jnp.sum(scaled, axis=-1, keepdims=True))


def tail_kernel(r_ref, even_ref, odd_ref, gs_ref, own_ref, place_ref, rs_ref, t_ref, loss_ref, g_ref, table_ref):
    first = dot_exact(even_ref[...], r_ref[...])
    second = dot_exact(odd_ref[...], r_ref[...])
    teacher = jnp.concatenate([first[:, :POOL], second[:, :POOL]], axis=1)
    student = jnp.concatenate([first[:, POOL:], second[:, POOL:]], axis=1)
    valid = teacher > 0.5 * low_score
    log_t = log_probs(teacher, valid)
    log_s = log_probs(student, valid)
    prob_t = jnp.where(valid, jnp.exp(log_t), 0.0)
    prob_s = jnp.where(valid, jnp.exp(log_s), 0.0)
    loss = jnp.sum(jnp.where(valid, prob_t * (log_t - log_s), 0.0), axis=-1, keepdims=True)
    grad = prob_s - prob_t
    kept = jnp.where(valid, teacher, 0.0)
    own = own_ref[...]
    mine = dot_exact(own, kept)
    t_ref[...] = dot_exact(mine, place_ref[...])
    loss_ref[...] = dot_exact(own, jnp.broadcast_to(loss, (loss.shape[0], LANES)))
    gs = gs_ref[...]
    g = student_scale * (dot_exact(gs[:8], grad[:, :POOL]) + dot_exact(gs[8:16], grad[:, POOL:]))
    g_ref[...] = g
    pool_student = jnp.concatenate(
        [rs_ref[:, POOL + t * PDEV : POOL + (t + 1) * PDEV, :].astype(f32).reshape(POOL, LANES) for t in range(8)],
        axis=1,
    ).astype(bf16)
    top = g.astype(bf16)
    mid = (g - top.astype(f32)).astype(bf16)
    term = dot32(top, pool_student) + dot32(mid, pool_student)
    back = (gs[:8] + gs[8:16]).T
    table_ref[...] = sum(back[:, j : j + 1] * term[j : j + 1] for j in range(HOLD_CAP))


def local(
    query_kv,
    student_query,
    block_holder,
    cand_local,
    counts,
    passage_qkv,
    passage_resid,
    student_passage,
    w_o,
    ln_gain,
    ln_bias,
    w_dense,
    b_dense,
    w_out,
):
    i32 = jnp.int32
    zi, yi, gi = lax.axis_index("pa_0"), lax.axis_index("pa_1"), lax.axis_index("pb")
    column = zi * NY + yi
    nblk = 2 * NA
    slot_len = cand_local.shape[2]
    vmem = lambda mib: pltpu.CompilerParams(vmem_limit_bytes=mib << 20)

    kv = query_kv.reshape(8, 8, NG, LANES)
    kv = jnp.transpose(kv, (2, 0, 1, 3)).reshape(NG, 8, FEAT)
    sq = jnp.broadcast_to(student_query.reshape(1, 8, LANES), (NG, 8, LANES))
    kv = jnp.concatenate([kv, sq], axis=2).reshape(NG * NZ, 1, KVW)
    kv = exchange(kv, ("pb", "pa_0"))
    kv = to_all(kv.reshape(NG * NZ, KVW), "pa_1").reshape(NY * NG * NZ, KVW)

    holder = block_holder.reshape(1, nblk)
    holders = to_all(holder, "pb").reshape(NG, nblk)

    def ranks(h):
        before = jnp.arange(nblk)[:, None] > jnp.arange(nblk)[None, :]
        return jnp.sum(((h[:, :, None] == h[:, None, :]) & before).astype(i32), axis=2)

    rank_all = ranks(holders)
    target = jnp.arange(NZ, dtype=i32) * NY + yi
    pick = (holders[None, :, None, :] == target[:, None, None, None]) & (
        rank_all[None, :, None, :] == jnp.arange(HOLD_CAP, dtype=i32)[None, None, :, None]
    )
    named = jnp.sum(jnp.where(pick, jnp.arange(nblk, dtype=i32), 0), axis=3) // 2
    source = (named % NY) * (NG * NZ) + jnp.arange(NG, dtype=i32)[None, :, None] * NZ + named // NY
    chooser = (
        source.reshape(NZ * SLOTS, 1) == jnp.arange(NY * NG * NZ, dtype=i32)[None, :]
    ).astype(bf16)
    kv = dot32(chooser, kv).astype(bf16).reshape(NZ, SLOTS, KVW)
    kv = exchange(kv, "pa_0")
    sq_all = jnp.transpose(kv[:, :, FEAT:], (1, 0, 2)).reshape(SLOTS, FEAT)
    sq_own = lax.dynamic_slice_in_dim(sq_all, gi * HOLD_CAP, HOLD_CAP, 0)

    sent = pl.pallas_call(
        self_kernel,
        grid=(8,),
        in_specs=[
            pl.BlockSpec((PDEV, 3, TOK, LANES), lambda i: (0, 0, 0, i)),
            pl.BlockSpec((PDEV, FEAT), lambda i: (0, 0)),
            pl.BlockSpec((PDEV, FEAT), lambda i: (0, 0)),
        ],
        out_specs=pl.BlockSpec((1, SENT, LANES), lambda i: (i, 0, 0)),
        out_shape=jax.ShapeDtypeStruct((8, SENT, LANES), bf16),
        compiler_params=vmem(24),
        name="self_part",
    )(passage_qkv, passage_resid, student_passage)
    pool = exchange(sent, "pb")

    pooled = pl.pallas_call(
        cross_kernel,
        grid=(SLOTS // STEP,),
        in_specs=[
            pl.BlockSpec((8, SENT, LANES), lambda i: (0, 0, 0)),
            pl.BlockSpec((NZ, 1, STEP, KVW), lambda i: (0, i, 0, 0)),
        ],
        out_specs=pl.BlockSpec((STEP // HOLD_CAP, HOLD_CAP, POOL, LANES), lambda i: (i, 0, 0, 0)),
        out_shape=jax.ShapeDtypeStruct((NG, HOLD_CAP, POOL, LANES), bf16),
        scratch_shapes=[pltpu.VMEM((2, ROWS, LANES), f32), pltpu.VMEM((STEP, POOL, LANES), f32)],
        compiler_params=vmem(32),
        name="cross_part",
    )(pool, kv.reshape(NZ, SLOTS // STEP, STEP, KVW))
    pooled = exchange(pooled, "pb").reshape(8, HOLD_CAP * POOL, LANES)

    own_holder = holder[0]
    own_rank = ranks(holder)[0]
    block_ids = jnp.arange(nblk, dtype=i32)
    slot_hit = (own_holder[None, :] == column) & (own_rank[None, :] == jnp.arange(HOLD_CAP, dtype=i32)[:, None])
    slot_block = jnp.sum(jnp.where(slot_hit, block_ids[None, :], 0), axis=1)
    slot_live = jnp.any(slot_hit, axis=1)
    spot = jnp.where(
        block_ids[:, None] % 2 * slot_len + jnp.arange(slot_len, dtype=i32)[None, :]
        < jnp.repeat(counts, 2)[:, None],
        cand_local.reshape(nblk, slot_len),
        -1,
    )
    spot = jnp.sum(jnp.where(slot_hit[:, :, None], spot[None], 0), axis=1)
    valid = jnp.any(
        (spot[:, :, None] == jnp.arange(POOL, dtype=i32)) & slot_live[:, None, None], axis=1
    ).astype(f32)
    slot_of = own_holder * HOLD_CAP + own_rank
    table = (slot_of[:, None] == jnp.arange(NA * HOLD_CAP, dtype=i32)[None, :]).astype(f32).reshape(NA, 2, -1)
    hit = slot_hit.astype(f32).reshape(HOLD_CAP, NA, 2)
    gs = jnp.pad(jnp.transpose(hit, (2, 0, 1)), ((0, 0), (0, 4), (0, 0))).reshape(16, NA)
    own = jnp.broadcast_to((jnp.arange(NA) == column).astype(f32), (8, NA))
    own_cand = lax.dynamic_slice_in_dim(cand_local, column, 1, 0).reshape(2 * slot_len)
    where_at = (jnp.arange(2 * slot_len, dtype=i32) // slot_len) * POOL + own_cand
    place = (jnp.arange(2 * POOL, dtype=i32)[:, None] == where_at[None, :]).astype(f32)

    rs_spec = pl.BlockSpec((8, 2 * POOL, LANES), lambda i: (0, 2 * ROWS // (2 * POOL), 0))
    full = lambda *shape: pl.BlockSpec(shape, lambda i: (0,) * len(shape))
    rows = [a.reshape(1, FEAT) for a in (ln_gain, ln_bias, b_dense, w_out)]
    scores = pl.pallas_call(
        head_kernel,
        grid=(1,),
        in_specs=[full(8, HOLD_CAP * POOL, LANES), rs_spec, full(HOLD_CAP, FEAT), full(HOLD_CAP, POOL)]
        + [full(FEAT, FEAT)] * 2
        + [full(1, FEAT)] * 4,
        out_specs=full(HOLD_CAP, LANES),
        out_shape=jax.ShapeDtypeStruct((HOLD_CAP, LANES), f32),
        compiler_params=vmem(40),
        name="head_part",
    )(pooled, pool, sq_own, valid, w_o, w_dense, *rows)
    everyone = to_all(to_all(scores, "pa_1"), "pa_0").reshape(NA * HOLD_CAP, LANES)

    own_t, own_loss, grads, query_table = pl.pallas_call(
        tail_kernel,
        grid=(1,),
        in_specs=[
            full(NA * HOLD_CAP, LANES),
            full(NA, NA * HOLD_CAP),
            full(NA, NA * HOLD_CAP),
            full(16, NA),
            full(8, NA),
            full(2 * POOL, 2 * slot_len),
            rs_spec,
        ],
        out_specs=[full(8, 2 * slot_len), full(8, LANES), full(8, POOL), full(NA, FEAT)],
        out_shape=[
            jax.ShapeDtypeStruct((8, 2 * slot_len), f32),
            jax.ShapeDtypeStruct((8, LANES), f32),
            jax.ShapeDtypeStruct((8, POOL), f32),
            jax.ShapeDtypeStruct((NA, FEAT), f32),
        ],
        compiler_params=vmem(16),
        name="tail_part",
    )(everyone, table[:, 0], table[:, 1], gs, own, place, pool)

    inward = exchange(query_table.reshape(NZ, NY, FEAT), "pa_0").sum(axis=0)
    grad_query = exchange(inward.reshape(NY, 1, FEAT), "pa_1").sum(axis=0)
    for_owner = jnp.transpose(grads[:HOLD_CAP].reshape(HOLD_CAP, NG, PDEV), (1, 0, 2))
    from_groups = exchange(for_owner, "pb").reshape(SLOTS, PDEV)
    grad_passage = jnp.einsum(
        "sp,sd->pd", from_groups, sq_all.astype(f32), precision=lax.Precision.HIGHEST
    )
    return (own_t[:1], own_loss[0, :1], grad_query, grad_passage)


def solution(mesh):
    torus = Mesh(mesh.devices.reshape(mesh.shape["pb"], NZ, NY), ("pb", "pa_0", "pa_1"))
    in_specs = (
        P(PB_PA, None, None, None),
        P(PB_PA, None),
        P("pb", None, None),
        P("pb", None, None),
        P("pb"),
        P(PA_PB, None, None, None),
        P(PA_PB, None),
        P(PA_PB, None),
        P(),
        P(),
        P(),
        P(),
        P(),
        P(),
    )
    out_specs = (P(PB_PA, None), P(PB_PA), P(PB_PA, None), P(PA_PB, None))
    return jax.shard_map(local, mesh=torus, in_specs=in_specs, out_specs=out_specs, check_vma=False)
```
